512 devices in a mesh: dp: 64 (over y_hi, z, core), tensor: 8 (over x, y_lo).
Axes of the slice: x: 4, y: 4 (y_hi: 2, y_lo: 2; y = y_hi * 2 + y_lo), z: 16, core: 2. Of those that a mesh axis runs over, the one named last changes fastest.
Arguments:
- queries: bfloat16 [2048, 5120], P('dp', 'tensor'), may hold values from -8 to 8
- new_keys: bfloat16 [2048, 5120], P('dp', 'tensor'), may hold values from -8 to 8
- new_values: bfloat16 [2048, 5120], P('dp', 'tensor'), may hold values from -6 to 6
- key_pool: bfloat16 [1024, 16, 5120], P('dp', None, 'tensor'), may hold values from -6 to 6
- value_pool: bfloat16 [1024, 16, 5120], P('dp', None, 'tensor'), may hold values from -6 to 6
- page_table: int32 [128, 16], P('dp'), may hold values from 0 to 15, as said below
- lengths: int32 [128], P('dp'), may hold values from 1 to 240, as said below
- timesteps: int32 [128], replicated, may hold values from 0 to 49
- gate_table: float32 [50, 5120], P(None, 'dp'), may hold values from -4 to 4
- out_weight: bfloat16 [5120, 5120], P('tensor', 'dp'), may hold values from -0.078125 to 0.078125
- residual: bfloat16 [32, 64, 5120], P('tensor', None, 'dp'), may hold values from -1.5 to 1.5
Outputs:
- mixed: bfloat16 [32, 64, 5120], P('tensor', None, 'dp')
The draws below stay inside these ranges and needn't reach their ends.
Inputs may be any that keep to these rules, and one draw needn't show every extreme that they name: `page_table`: ids of pages within the 16-page pool of the request's own group; the first ceil(lengths[r] / 16) entries of the requests of one group are distinct pages, and together they take at most 16 pages; in every draw some group takes all 16. `lengths`: some request has exactly 240 cached positions in every draw.
All inputs are finite; a program needn't handle non-finite values.
Results may differ from the reference program's by a relative error of at most 0.0054.
Values may be sent and summed in bfloat16 or wider, within the bound.
No kernel may reach another device: no remote copies, remote signals or barrier semaphores. Data moves between devices by JAX's collectives and lax.ppermute only.
A program may use at most 64 MiB of HBM per device.

```python
import math
import jax
import jax.numpy as jnp
from jax import lax

D = 5120
HEADS = 40
HEAD = 128
NEW = 16
PAGE = 16
STEPS = 50
REQ_DEV = 2
P_DEV = 16
REQ = 128
TOKENS = 2048
GROUP_TOK = 32
GROUPS = 64
POOL = 1024


def span_pair(key):
    base = jax.random.fold_in(key, 17)
    key_query, key_new = jax.random.split(base, 2)
    width = HEADS * HEAD
    query_draw = jnp.clip(jax.random.normal(key_query, (REQ, NEW, width), jnp.float32), -6.0, 6.0)
    newk_draw = jnp.clip(jax.random.normal(key_new, (REQ, NEW, width), jnp.float32), -6.0, 6.0)
    return (query_draw.reshape(TOKENS, width), newk_draw.reshape(TOKENS, width))


def page_plan(key):
    base = jax.random.fold_in(key, 29)
    key_busy, key_shift, key_owner, key_tail, key_perm = jax.random.split(base, 5)
    groups = REQ // REQ_DEV
    busiest = jax.random.randint(key_busy, (), 0, groups)
    shifts = jax.random.randint(key_shift, (groups,), 0, 4)
    is_busy = jnp.arange(groups) == busiest
    totals = jnp.maximum(REQ_DEV, P_DEV // jnp.left_shift(1, shifts))
    totals = jnp.where(is_busy, P_DEV, totals)
    spare = totals - REQ_DEV
    owner = jax.random.randint(key_owner, (groups, P_DEV), 0, REQ_DEV)
    live = jnp.arange(P_DEV)[None, :] < spare[:, None]
    picked = (owner[:, :, None] == jnp.arange(REQ_DEV)[None, None, :]) & live[:, :, None]
    counts = 1 + jnp.sum(picked.astype(jnp.int32), axis=1)
    busy_counts = jnp.where(jnp.arange(REQ_DEV) == 0, P_DEV - REQ_DEV + 1, 1)
    counts = jnp.where(is_busy[:, None], busy_counts[None, :], counts)
    tails = jax.random.randint(key_tail, (groups, REQ_DEV), 1, PAGE + 1)
    first_full = is_busy[:, None] & (jnp.arange(REQ_DEV)[None, :] == 0)
    tails = jnp.where(first_full, PAGE, tails)
    length_draw = (counts - 1) * PAGE + tails
    offsets = jnp.cumsum(counts, axis=1) - counts
    orders = jax.vmap(lambda subkey: jax.random.permutation(subkey, P_DEV))(jax.random.split(key_perm, groups))
    slots = (offsets[:, :, None] + jnp.arange(P_DEV)[None, None, :]) % P_DEV
    table = orders[jnp.arange(groups)[:, None, None], slots]
    return (table.reshape(REQ, P_DEV).astype(jnp.int32), length_draw.reshape(REQ).astype(jnp.int32))


def draw_queries(key, part):
    return span_pair(key)[0].astype(jnp.bfloat16)


def draw_new_keys(key, part):
    return span_pair(key)[1].astype(jnp.bfloat16)


def draw_page_table(key, part):
    return page_plan(key)[0]


def draw_lengths(key, part):
    return page_plan(key)[1]


def place_ends(entries, rng, least, top_value):
    spot = [jax.random.randint(jax.random.fold_in(rng, axis), (), 0, length) for axis, length in enumerate(entries.shape)]
    main_axis = entries.shape.index(max(entries.shape))
    beside = spot[:main_axis] + [(spot[main_axis] + 1) % entries.shape[main_axis]] + spot[main_axis + 1:]
    return entries.at[tuple(spot)].set(least).at[tuple(beside)].set(top_value)


def block_scale(key, extent, cuts, least, high):
    factor_of, own = 1.0, jax.random.fold_in(key, 6)
    for dim, shards_of in cuts:
        draws = jnp.exp(jax.random.uniform(jax.random.fold_in(own, dim), (shards_of,), jnp.float32, least / len(cuts), high / len(cuts)))
        factor_of = factor_of * jnp.repeat(draws, extent[dim] // shards_of).reshape([-1 if axis == dim else 1 for axis in range(len(extent))])
    return factor_of


def noise(rng, extent, scale, bound, cuts=(), kind=jnp.bfloat16):
    array = scale * jax.random.normal(rng, extent, jnp.float32)
    if cuts:
        array = array * block_scale(rng, extent, cuts, -0.22, 0.18)
    return jnp.clip(array, -bound, bound).astype(kind)


def setup_inputs(seed: int = 0) -> dict:
    key_of = jax.random.split(jax.random.key(seed), 12)
    queries = draw_queries(jax.random.fold_in(key_of[11], 71), 0)
    new_keys = draw_new_keys(jax.random.fold_in(key_of[11], 71), 0)
    new_values = noise(key_of[2], (TOKENS, HEADS * HEAD), 1.0, 6.0, ((0, 64), (1, 8)))
    key_pool = noise(key_of[3], (POOL, PAGE, HEADS * HEAD), 1.0, 6.0, ((0, 64), (2, 8)))
    value_pool = noise(key_of[4], (POOL, PAGE, HEADS * HEAD), 1.0, 6.0, ((0, 64), (2, 8)))
    page_table = draw_page_table(jax.random.fold_in(key_of[11], 71), 0)
    lengths = draw_lengths(jax.random.fold_in(key_of[11], 71), 0)
    timesteps = place_ends(jax.random.randint(key_of[7], (REQ,), 0, STEPS), jax.random.fold_in(key_of[7], 1), 0, STEPS - 1).astype(jnp.int32)
    gate_table = noise(key_of[8], (STEPS, D), 1.0, 4.0, ((1, 64),), jnp.float32)
    out_weight = noise(key_of[9], (HEADS * HEAD, D), (HEADS * HEAD) ** -0.5, 0.078125, ((0, 8), (1, 64)))
    residual = noise(key_of[10], (GROUP_TOK, GROUPS, D), 0.25, 1.5, ((0, 8), (2, 64)))
    return dict(queries=queries, new_keys=new_keys, new_values=new_values, key_pool=key_pool, value_pool=value_pool, page_table=page_table, lengths=lengths, timesteps=timesteps, gate_table=gate_table, out_weight=out_weight, residual=residual)


def reference(queries, new_keys, new_values, key_pool, value_pool, page_table, lengths, timesteps, gate_table, out_weight, residual):
    groups = REQ // REQ_DEV
    width = HEADS * HEAD
    cached = P_DEV * PAGE
    group_tok = REQ_DEV * NEW

    def per_group(items):
        query_g, newk_g, newv_g, kpool_g, vpool_g, table_g, length_g = items
        keys_ctx = kpool_g[table_g].reshape(REQ_DEV, cached, width)
        vals_ctx = vpool_g[table_g].reshape(REQ_DEV, cached, width)
        keys_all = jnp.concatenate([keys_ctx, newk_g.reshape(REQ_DEV, NEW, width)], axis=1)
        vals_all = jnp.concatenate([vals_ctx, newv_g.reshape(REQ_DEV, NEW, width)], axis=1)
        keys_all = keys_all.reshape(REQ_DEV, cached + NEW, HEADS, HEAD).astype(jnp.float32)
        vals_all = vals_all.reshape(REQ_DEV, cached + NEW, HEADS, HEAD).astype(jnp.float32)
        query_four = query_g.reshape(REQ_DEV, NEW, HEADS, HEAD).astype(jnp.float32)
        scores = jnp.einsum('rqhd,rkhd->rhqk', query_four, keys_all) * (1.0 / math.sqrt(HEAD))
        position = jnp.arange(cached + NEW)
        visible = (position[None, :] < length_g[:, None]) | (position[None, :] >= cached)
        scores = jnp.where(visible[:, None, None, :], scores, jnp.float32(-1e+30))
        top = lax.optimization_barrier(jnp.max(scores, axis=-1, keepdims=True))
        expd = jnp.exp(scores - top)
        probs = (expd / lax.optimization_barrier(jnp.sum(expd, axis=-1, keepdims=True))).astype(jnp.bfloat16)
        mixed_heads = jnp.einsum('rhqk,rkhd->rqhd', probs.astype(jnp.float32), vals_all)
        return mixed_heads.astype(jnp.bfloat16).reshape(group_tok, width)
    stacked = (queries.reshape(groups, group_tok, width), new_keys.reshape(groups, group_tok, width), new_values.reshape(groups, group_tok, width), key_pool.reshape(groups, P_DEV, PAGE, width), value_pool.reshape(groups, P_DEV, PAGE, width), page_table.reshape(groups, REQ_DEV, P_DEV), lengths.reshape(groups, REQ_DEV))
    attn = lax.map(per_group, stacked).reshape(TOKENS, width)
    branch = jnp.dot(attn, out_weight, preferred_element_type=jnp.float32)
    step_rows = jnp.repeat(timesteps, NEW)
    gate = gate_table[step_rows]
    stream = jnp.transpose(residual, (1, 0, 2)).reshape(TOKENS, D).astype(jnp.float32)
    total = (stream + gate * branch).astype(jnp.bfloat16)
    return jnp.transpose(total.reshape(groups, group_tok, D), (1, 0, 2))
```

```python
import math

import jax
import jax.numpy as jnp
from jax import lax
from jax.sharding import Mesh
from jax.sharding import PartitionSpec as P

HEAD = 128


def attend(queries, new_keys, new_values, key_pool, value_pool, page_table, lengths):
    req_dev = page_table.shape[0]
    pages, page_len, width = key_pool.shape
    tok_count = queries.shape[0]
    new_count = tok_count // req_dev
    heads_dev = width // HEAD
    cached = pages * page_len
    keys_all = jnp.concatenate(
        [
            key_pool[page_table].reshape(req_dev, cached, width),
            new_keys.reshape(req_dev, new_count, width),
        ],
        axis=1,
    )
    vals_all = jnp.concatenate(
        [
            value_pool[page_table].reshape(req_dev, cached, width),
            new_values.reshape(req_dev, new_count, width),
        ],
        axis=1,
    )
    keys_all = keys_all.reshape(req_dev, cached + new_count, heads_dev, HEAD)
    vals_all = vals_all.reshape(req_dev, cached + new_count, heads_dev, HEAD)
    query_four = queries.reshape(req_dev, new_count, heads_dev, HEAD)
    scores = jnp.einsum(
        "rqhd,rkhd->rhqk", query_four, keys_all, preferred_element_type=jnp.float32
    ) * (1.0 / math.sqrt(HEAD))
    position = jnp.arange(cached + new_count)
    visible = (position[None, :] < lengths[:, None]) | (position[None, :] >= cached)
    scores = jnp.where(visible[:, None, None, :], scores, jnp.float32(-1e30))
    top = jnp.max(scores, axis=-1, keepdims=True)
    expd = jnp.exp(scores - top)
    probs = (expd / jnp.sum(expd, axis=-1, keepdims=True)).astype(jnp.bfloat16)
    mixed_heads = jnp.einsum("rhqk,rkhd->rqhd", probs, vals_all, preferred_element_type=jnp.float32)
    return mixed_heads.astype(jnp.bfloat16).reshape(tok_count, width)


def per_device(
    queries,
    new_keys,
    new_values,
    key_pool,
    value_pool,
    page_table,
    lengths,
    timesteps,
    gate_table,
    out_weight,
    residual,
):
    req_dev = page_table.shape[0]
    group_tok = queries.shape[0]
    new_count = group_tok // req_dev
    share = residual.shape[0]
    groups = residual.shape[1]
    col_count = out_weight.shape[1]
    y_hi, z_len, cores = (lax.axis_size(name) for name in ("y_hi", "z", "core"))
    tensor_len = lax.axis_size("x") * lax.axis_size("y_lo")
    weight = lax.all_gather(out_weight, ("y_hi", "core"), axis=1, tiled=True)
    attn = attend(queries, new_keys, new_values, key_pool, value_pool, page_table, lengths)
    attn_all = lax.all_gather(attn, "z", axis=0, tiled=True)
    partial = jnp.dot(attn_all, weight, preferred_element_type=jnp.float32).astype(jnp.bfloat16)
    blocks = partial.reshape(z_len, tensor_len, share, y_hi * cores, col_count)
    blocks = blocks.transpose(3, 1, 0, 2, 4).reshape(-1, z_len, share, col_count)
    arrived = lax.all_to_all(blocks, ("y_hi", "core", "x", "y_lo"), 0, 0, tiled=True)
    arrived = arrived.reshape(y_hi, cores, tensor_len, z_len, share, col_count)
    branch = jnp.sum(arrived.astype(jnp.float32), axis=2)
    branch = branch.transpose(3, 0, 2, 1, 4).reshape(share, groups, col_count)
    tensor_at = lax.axis_index(("x", "y_lo"))
    local_rows = tensor_at * share + jnp.arange(share, dtype=jnp.int32)
    request_at = (
        jnp.arange(groups, dtype=jnp.int32)[None, :] * req_dev + (local_rows // new_count)[:, None]
    )
    step_at = timesteps[request_at]
    onehot = (
        step_at[:, :, None] == jnp.arange(gate_table.shape[0], dtype=jnp.int32)[None, None, :]
    ).astype(jnp.float32)
    gate = jnp.einsum("tgs,sc->tgc", onehot, gate_table, precision=lax.Precision.HIGHEST)
    return (residual.astype(jnp.float32) + gate * branch).astype(jnp.bfloat16)


def solution(mesh):
    dp = ("y_hi", "z", "core")
    tensor = ("x", "y_lo")
    split = Mesh(mesh.devices.reshape(2, -1, 2, 4, 2), dp + tensor)
    placed = (
        P(dp, tensor),
        P(dp, tensor),
        P(dp, tensor),
        P(dp, None, tensor),
        P(dp, None, tensor),
        P(dp, None),
        P(dp),
        P(),
        P(None, dp),
        P(tensor, dp),
        P(tensor, None, dp),
    )
    return jax.shard_map(
        per_device, mesh=split, in_specs=placed, out_specs=P(tensor, None, dp), check_vma=False
    )
```

```python
import math

import jax
import jax.numpy as jnp
from jax import lax
from jax.experimental import pallas as pl
from jax.experimental.pallas import tpu as pltpu
from jax.sharding import Mesh
from jax.sharding import PartitionSpec as P

HEAD = 128
HIDDEN = -1e30


def nt_dot(left, right):
    return lax.dot_general(left, right, (((1,), (1,)), ((), ())), preferred_element_type=jnp.float32)


def attend_kernel(table, lengths, query, new_key, new_value, key_pool, value_pool, out):
    req_dev, pages = table.shape
    tok_count, width = query.shape
    cached = key_pool.shape[0]
    page_len = cached // pages
    new_count = tok_count // req_dev
    slot = lax.broadcasted_iota(jnp.int32, (1, cached), 1)
    page = slot // page_len
    inner = slot - page * page_len
    row_req = lax.broadcasted_iota(jnp.int32, (tok_count, 1), 0) // new_count
    seen = jnp.zeros((tok_count, cached), jnp.int32)
    for req in range(req_dev):
        left = jnp.zeros((1, cached), jnp.int32)
        for entry in range(pages):
            left = jnp.where(
                page == table[req, entry], jnp.maximum(left, lengths[req] - entry * page_len), left
            )
        seen = jnp.where(row_req == req, (inner < left).astype(jnp.int32), seen)
    new_req = lax.broadcasted_iota(jnp.int32, (1, tok_count), 1) // new_count
    own = row_req == new_req
    pool_seen = seen > 0
    scale = 1.0 / math.sqrt(HEAD)
    for head in range(width // HEAD):
        at = slice(head * HEAD, (head + 1) * HEAD)
        q = query[:, at]
        pool_score = jnp.where(pool_seen, nt_dot(q, key_pool[:, at]) * scale, HIDDEN)
        new_score = jnp.where(own, nt_dot(q, new_key[:, at]) * scale, HIDDEN)
        top = jnp.maximum(
            jnp.max(pool_score, axis=1, keepdims=True), jnp.max(new_score, axis=1, keepdims=True)
        )
        pool_exp = jnp.exp(pool_score - top)
        new_exp = jnp.exp(new_score - top)
        total = jnp.sum(pool_exp, axis=1, keepdims=True) + jnp.sum(new_exp, axis=1, keepdims=True)
        mixed = jnp.dot(
            (pool_exp / total).astype(jnp.bfloat16),
            value_pool[:, at],
            preferred_element_type=jnp.float32,
        ) + jnp.dot(
            (new_exp / total).astype(jnp.bfloat16),
            new_value[:, at],
            preferred_element_type=jnp.float32,
        )
        out[:, at] = mixed.astype(jnp.bfloat16)


def attend(queries, new_keys, new_values, key_pool, value_pool, page_table, lengths, interpret=False):
    smem = pl.BlockSpec(memory_space=pltpu.SMEM)
    vmem = pl.BlockSpec(memory_space=pltpu.VMEM)
    width = queries.shape[1]
    return pl.pallas_call(
        attend_kernel,
        out_shape=jax.ShapeDtypeStruct(queries.shape, jnp.bfloat16),
        in_specs=[smem, smem] + [vmem] * 5,
        out_specs=vmem,
        interpret=interpret,
        name="attend",
    )(
        page_table,
        lengths,
        queries,
        new_keys,
        new_values,
        key_pool.reshape(-1, width),
        value_pool.reshape(-1, width),
    )


def per_device(
    queries,
    new_keys,
    new_values,
    key_pool,
    value_pool,
    page_table,
    lengths,
    timesteps,
    gate_table,
    out_weight,
    residual,
):
    req_dev = page_table.shape[0]
    group_tok = queries.shape[0]
    new_count = group_tok // req_dev
    share = residual.shape[0]
    groups = residual.shape[1]
    col_count = out_weight.shape[1]
    y_hi, z_len, cores = (lax.axis_size(name) for name in ("y_hi", "z", "core"))
    tensor_len = lax.axis_size("x") * lax.axis_size("y_lo")
    own_columns = jnp.broadcast_to(out_weight.T[None], (y_hi * cores, col_count, out_weight.shape[0]))
    weight = lax.all_to_all(own_columns, ("y_hi", "core"), 0, 0, tiled=True)
    weight = weight.reshape(-1, out_weight.shape[0])
    attn = attend(queries, new_keys, new_values, key_pool, value_pool, page_table, lengths)
    attn_all = lax.all_gather(attn, "z", axis=0, tiled=True)
    partial = nt_dot(attn_all, weight).astype(jnp.bfloat16)
    blocks = partial.reshape(z_len, tensor_len, share, y_hi * cores, col_count)
    blocks = blocks.transpose(3, 1, 0, 2, 4).reshape(-1, z_len, share, col_count)
    arrived = lax.all_to_all(blocks, ("y_hi", "core", "x", "y_lo"), 0, 0, tiled=True)
    arrived = arrived.reshape(y_hi, cores, tensor_len, z_len, share, col_count)
    branch = jnp.sum(arrived.astype(jnp.float32), axis=2)
    branch = branch.transpose(3, 0, 2, 1, 4).reshape(share, groups, col_count)
    tensor_at = lax.axis_index(("x", "y_lo"))
    local_rows = tensor_at * share + jnp.arange(share, dtype=jnp.int32)
    request_at = (
        jnp.arange(groups, dtype=jnp.int32)[None, :] * req_dev + (local_rows // new_count)[:, None]
    )
    step_at = timesteps[request_at]
    onehot = (
        step_at[:, :, None] == jnp.arange(gate_table.shape[0], dtype=jnp.int32)[None, None, :]
    ).astype(jnp.float32)
    gate = jnp.einsum("tgs,sc->tgc", onehot, gate_table, precision=lax.Precision.HIGHEST)
    return (residual.astype(jnp.float32) + gate * branch).astype(jnp.bfloat16)


def solution(mesh):
    dp = ("y_hi", "z", "core")
    tensor = ("x", "y_lo")
    split = Mesh(mesh.devices.reshape(2, -1, 2, 4, 2), dp + tensor)
    placed = (
        P(dp, tensor),
        P(dp, tensor),
        P(dp, tensor),
        P(dp, None, tensor),
        P(dp, None, tensor),
        P(dp, None),
        P(dp),
        P(),
        P(None, dp),
        P(tensor, dp),
        P(tensor, None, dp),
    )
    return jax.shard_map(
        per_device, mesh=split, in_specs=placed, out_specs=P(tensor, None, dp), check_vma=False
    )
```

```python
import math

import jax
import jax.numpy as jnp
from jax import lax
from jax.experimental import pallas as pl
from jax.experimental.pallas import tpu as pltpu
from jax.sharding import Mesh
from jax.sharding import PartitionSpec as P

HEAD = 128
HIDDEN = -1e30


def nt_dot(left, right):
    return lax.dot_general(left, right, (((1,), (1,)), ((), ())), preferred_element_type=jnp.float32)


def attend_kernel(table, lengths, query, new_key, new_value, key_pool, value_pool, out):
    req_dev, pages = table.shape
    tok_count, width = query.shape
    cached = key_pool.shape[0]
    page_len = cached // pages
    new_count = tok_count // req_dev
    slot = lax.broadcasted_iota(jnp.int32, (1, cached), 1)
    page = slot // page_len
    inner = slot - page * page_len
    row_req = lax.broadcasted_iota(jnp.int32, (tok_count, 1), 0) // new_count
    seen = jnp.zeros((tok_count, cached), jnp.int32)
    for req in range(req_dev):
        left = jnp.zeros((1, cached), jnp.int32)
        for entry in range(pages):
            left = jnp.where(
                page == table[req, entry], jnp.maximum(left, lengths[req] - entry * page_len), left
            )
        seen = jnp.where(row_req == req, (inner < left).astype(jnp.int32), seen)
    new_req = lax.broadcasted_iota(jnp.int32, (1, tok_count), 1) // new_count
    own = row_req == new_req
    pool_seen = seen > 0
    scale = 1.0 / math.sqrt(HEAD)
    for head in range(width // HEAD):
        at = slice(head * HEAD, (head + 1) * HEAD)
        q = query[:, at]
        pool_score = jnp.where(pool_seen, nt_dot(q, key_pool[:, at]) * scale, HIDDEN)
        new_score = jnp.where(own, nt_dot(q, new_key[:, at]) * scale, HIDDEN)
        top = jnp.maximum(
            jnp.max(pool_score, axis=1, keepdims=True), jnp.max(new_score, axis=1, keepdims=True)
        )
        pool_exp = jnp.exp(pool_score - top)
        new_exp = jnp.exp(new_score - top)
        total = jnp.sum(pool_exp, axis=1, keepdims=True) + jnp.sum(new_exp, axis=1, keepdims=True)
        mixed = jnp.dot(
            (pool_exp / total).astype(jnp.bfloat16),
            value_pool[:, at],
            preferred_element_type=jnp.float32,
        ) + jnp.dot(
            (new_exp / total).astype(jnp.bfloat16),
            new_value[:, at],
            preferred_element_type=jnp.float32,
        )
        out[:, at] = mixed.astype(jnp.bfloat16)


def attend(queries, new_keys, new_values, key_pool, value_pool, page_table, lengths, interpret=False):
    smem = pl.BlockSpec(memory_space=pltpu.SMEM)
    vmem = pl.BlockSpec(memory_space=pltpu.VMEM)
    width = queries.shape[1]
    return pl.pallas_call(
        attend_kernel,
        out_shape=jax.ShapeDtypeStruct(queries.shape, jnp.bfloat16),
        in_specs=[smem, smem] + [vmem] * 5,
        out_specs=vmem,
        interpret=interpret,
        name="attend",
    )(
        page_table,
        lengths,
        queries,
        new_keys,
        new_values,
        key_pool.reshape(-1, width),
        value_pool.reshape(-1, width),
    )


def project_kernel(attn, weight, out, packed):
    blocks, tensor_len, rows, lanes = out.shape
    cols = weight.shape[0] // blocks
    half = attn.shape[0] // 2
    share = half // (tensor_len * rows)
    to = lax.broadcasted_iota(jnp.int32, (half, half), 0)
    source = (
        (to % rows) * (tensor_len * share)
        + (to // rows) % tensor_len * share
        + to // (rows * tensor_len)
    )
    order = (source == lax.broadcasted_iota(jnp.int32, (half, half), 1)).astype(jnp.bfloat16)
    sorted_rows = [
        jnp.dot(
            order, attn[part * half : (part + 1) * half, :], preferred_element_type=jnp.float32
        ).astype(jnp.bfloat16)
        for part in range(2)
    ]
    run = tensor_len * rows
    for block in range(blocks):
        block_weight = weight[block * cols : (block + 1) * cols, :]
        for part in range(2):
            partial = nt_dot(sorted_rows[part], block_weight)
            for row in range(share):
                at = (part * share + row) * cols
                packed[:, at : at + cols] = partial[row * run : (row + 1) * run]
        out[block] = packed[...].astype(jnp.bfloat16).reshape(tensor_len, rows, lanes)


def project(attn, weight, blocks, tensor_len, interpret=False):
    cols = weight.shape[0] // blocks
    rows = 8
    lanes = attn.shape[0] // (tensor_len * rows) * cols
    vmem = pl.BlockSpec(memory_space=pltpu.VMEM)
    return pl.pallas_call(
        project_kernel,
        out_shape=jax.ShapeDtypeStruct((blocks, tensor_len, rows, lanes), jnp.bfloat16),
        in_specs=[vmem, vmem],
        out_specs=vmem,
        scratch_shapes=[pltpu.VMEM((tensor_len * rows, lanes), jnp.float32)],
        interpret=interpret,
        name="project",
    )(attn, weight)


def finish_kernel(arrived, gate, residual, out, branch):
    y_hi, cores, tensor_len, rows, lanes = arrived.shape
    share, groups, cols = residual.shape
    for side in range(y_hi):
        for core in range(cores):
            total = jnp.sum(arrived[side, core].astype(jnp.float32), axis=0)
            for place in range(lanes // cols):
                first = (side * (groups // y_hi)) + (place // share) * rows * cores + core
                branch[place % share, pl.ds(first, rows, cores), :] = total[
                    :, place * cols : (place + 1) * cols
                ]
    for row in range(share):
        out[row] = (residual[row].astype(jnp.float32) + gate[...] * branch[row]).astype(jnp.bfloat16)


def finish(arrived, gate, residual, interpret=False):
    vmem = pl.BlockSpec(memory_space=pltpu.VMEM)
    return pl.pallas_call(
        finish_kernel,
        out_shape=jax.ShapeDtypeStruct(residual.shape, residual.dtype),
        in_specs=[vmem, vmem, vmem],
        out_specs=vmem,
        scratch_shapes=[pltpu.VMEM(residual.shape, jnp.float32)],
        interpret=interpret,
        name="finish",
    )(arrived, gate, residual)


def per_device(
    queries,
    new_keys,
    new_values,
    key_pool,
    value_pool,
    page_table,
    lengths,
    timesteps,
    gate_table,
    out_weight,
    residual,
):
    req_dev = page_table.shape[0]
    group_tok = queries.shape[0]
    new_count = group_tok // req_dev
    share = residual.shape[0]
    groups = residual.shape[1]
    col_count = out_weight.shape[1]
    y_hi, cores = (lax.axis_size(name) for name in ("y_hi", "core"))
    tensor_len = lax.axis_size("x") * lax.axis_size("y_lo")
    own_columns = jnp.broadcast_to(out_weight.T[None], (y_hi * cores, col_count, out_weight.shape[0]))
    weight = lax.all_to_all(own_columns, ("y_hi", "core"), 0, 0, tiled=True)
    weight = weight.reshape(-1, out_weight.shape[0])
    attn = attend(queries, new_keys, new_values, key_pool, value_pool, page_table, lengths)
    attn_all = lax.all_gather(attn, "z", axis=0, tiled=True)
    blocks = project(attn_all, weight, y_hi * cores, tensor_len)
    blocks = blocks.reshape(-1, *blocks.shape[2:])
    arrived = lax.all_to_all(blocks, ("y_hi", "core", "x", "y_lo"), 0, 0, tiled=True)
    request_at = lax.axis_index(("x", "y_lo")) * share // new_count
    step_at = lax.dynamic_index_in_dim(timesteps.reshape(groups, req_dev), request_at, 1, False)
    onehot = (step_at[:, None] == jnp.arange(gate_table.shape[0], dtype=jnp.int32)[None, :]).astype(
        jnp.float32
    )
    gate = jnp.dot(onehot, gate_table, precision=lax.Precision.HIGHEST)
    return finish(arrived.reshape(y_hi, cores, tensor_len, *arrived.shape[1:]), gate, residual)


def solution(mesh):
    dp = ("y_hi", "z", "core")
    tensor = ("x", "y_lo")
    split = Mesh(mesh.devices.reshape(2, -1, 2, 4, 2), dp + tensor)
    placed = (
        P(dp, tensor),
        P(dp, tensor),
        P(dp, tensor),
        P(dp, None, tensor),
        P(dp, None, tensor),
        P(dp, None),
        P(dp),
        P(),
        P(None, dp),
        P(tensor, dp),
        P(tensor, None, dp),
    )
    return jax.shard_map(
        per_device, mesh=split, in_specs=placed, out_specs=P(tensor, None, dp), check_vma=False
    )
```

```python
import math

import jax
import jax.numpy as jnp
from jax import lax
from jax.experimental import pallas as pl
from jax.experimental.pallas import tpu as pltpu
from jax.sharding import Mesh
from jax.sharding import PartitionSpec as P

HEAD = 128
HIDDEN = -1e30
SMALL = pltpu.CompilerParams(vmem_limit_bytes=12 * 1024 * 1024)


def nt_dot(left, right):
    return lax.dot_general(left, right, (((1,), (1,)), ((), ())), preferred_element_type=jnp.float32)


def attend_kernel(table, lengths, query, new_key, new_value, key_pool, value_pool, out):
    req_dev, pages = table.shape
    tok_count, width = query.shape
    cached = key_pool.shape[0]
    page_len = cached // pages
    new_count = tok_count // req_dev
    slot = lax.broadcasted_iota(jnp.int32, (1, cached), 1)
    page = slot // page_len
    inner = slot - page * page_len
    row_req = lax.broadcasted_iota(jnp.int32, (tok_count, 1), 0) // new_count
    seen = jnp.zeros((tok_count, cached), jnp.int32)
    for req in range(req_dev):
        left = jnp.zeros((1, cached), jnp.int32)
        for entry in range(pages):
            left = jnp.where(
                page == table[req, entry], jnp.maximum(left, lengths[req] - entry * page_len), left
            )
        seen = jnp.where(row_req == req, (inner < left).astype(jnp.int32), seen)
    new_req = lax.broadcasted_iota(jnp.int32, (1, tok_count), 1) // new_count
    own = row_req == new_req
    pool_seen = seen > 0
    scale = 1.0 / math.sqrt(HEAD)
    for head in range(width // HEAD):
        at = slice(head * HEAD, (head + 1) * HEAD)
        q = query[:, at]
        pool_score = jnp.where(pool_seen, nt_dot(q, key_pool[:, at]) * scale, HIDDEN)
        new_score = jnp.where(own, nt_dot(q, new_key[:, at]) * scale, HIDDEN)
        top = jnp.maximum(
            jnp.max(pool_score, axis=1, keepdims=True), jnp.max(new_score, axis=1, keepdims=True)
        )
        pool_exp = jnp.exp(pool_score - top)
        new_exp = jnp.exp(new_score - top)
        total = jnp.sum(pool_exp, axis=1, keepdims=True) + jnp.sum(new_exp, axis=1, keepdims=True)
        mixed = jnp.dot(
            (pool_exp / total).astype(jnp.bfloat16),
            value_pool[:, at],
            preferred_element_type=jnp.float32,
        ) + jnp.dot(
            (new_exp / total).astype(jnp.bfloat16),
            new_value[:, at],
            preferred_element_type=jnp.float32,
        )
        out[:, at] = mixed.astype(jnp.bfloat16)


def attend(queries, new_keys, new_values, key_pool, value_pool, page_table, lengths, interpret=False):
    smem = pl.BlockSpec(memory_space=pltpu.SMEM)
    vmem = pl.BlockSpec(memory_space=pltpu.VMEM)
    width = queries.shape[1]
    return pl.pallas_call(
        attend_kernel,
        out_shape=jax.ShapeDtypeStruct(queries.shape, jnp.bfloat16),
        in_specs=[smem, smem] + [vmem] * 5,
        out_specs=vmem,
        interpret=interpret,
        compiler_params=SMALL,
        name="attend",
    )(
        page_table,
        lengths,
        queries,
        new_keys,
        new_values,
        key_pool.reshape(-1, width),
        value_pool.reshape(-1, width),
    )


def project_kernel(attn, weight, out, packed):
    blocks, tensor_len, rows, lanes = out.shape
    cols = weight.shape[0] // blocks
    half = attn.shape[0] // 2
    share = half // (tensor_len * rows)
    to = lax.broadcasted_iota(jnp.int32, (half, 1), 0)
    row_bits, tensor_bits = rows.bit_length() - 1, tensor_len.bit_length() - 1
    row_at = to & (rows - 1)
    tensor_at = (to >> row_bits) & (tensor_len - 1)
    share_at = to >> (row_bits + tensor_bits)
    source = (row_at * tensor_len + tensor_at) * share + share_at
    order = (source == lax.broadcasted_iota(jnp.int32, (half, half), 1)).astype(jnp.bfloat16)
    sorted_rows = [
        jnp.dot(
            order, attn[part * half : (part + 1) * half, :], preferred_element_type=jnp.float32
        ).astype(jnp.bfloat16)
        for part in range(2)
    ]
    run = tensor_len * rows
    for block in range(blocks):
        block_weight = weight[block * cols : (block + 1) * cols, :]
        for part in range(2):
            partial = nt_dot(sorted_rows[part], block_weight)
            for row in range(share):
                at = (part * share + row) * cols
                packed[:, at : at + cols] = partial[row * run : (row + 1) * run]
        out[block] = packed[...].astype(jnp.bfloat16).reshape(tensor_len, rows, lanes)


def project(attn, weight, blocks, tensor_len, interpret=False):
    cols = weight.shape[0] // blocks
    rows = 8
    lanes = attn.shape[0] // (tensor_len * rows) * cols
    vmem = pl.BlockSpec(memory_space=pltpu.VMEM)
    return pl.pallas_call(
        project_kernel,
        out_shape=jax.ShapeDtypeStruct((blocks, tensor_len, rows, lanes), jnp.bfloat16),
        in_specs=[vmem, vmem],
        out_specs=vmem,
        scratch_shapes=[pltpu.VMEM((tensor_len * rows, lanes), jnp.float32)],
        interpret=interpret,
        compiler_params=SMALL,
        name="project",
    )(attn, weight)


def finish_kernel(arrived, gate, residual, out, branch):
    y_hi, cores, tensor_len, rows, lanes = arrived.shape
    share, groups, cols = residual.shape
    for side in range(y_hi):
        for core in range(cores):
            total = jnp.sum(arrived[side, core].astype(jnp.float32), axis=0)
            for place in range(lanes // cols):
                first = (side * (groups // y_hi)) + (place // share) * rows * cores + core
                branch[place % share, pl.ds(first, rows, cores), :] = total[
                    :, place * cols : (place + 1) * cols
                ]
    for row in range(share):
        out[row] = (residual[row].astype(jnp.float32) + gate[...] * branch[row]).astype(jnp.bfloat16)


def finish(arrived, gate, residual, interpret=False):
    vmem = pl.BlockSpec(memory_space=pltpu.VMEM)
    return pl.pallas_call(
        finish_kernel,
        out_shape=jax.ShapeDtypeStruct(residual.shape, residual.dtype),
        in_specs=[vmem, vmem, vmem],
        out_specs=vmem,
        scratch_shapes=[pltpu.VMEM(residual.shape, jnp.float32)],
        interpret=interpret,
        compiler_params=SMALL,
        name="finish",
    )(arrived, gate, residual)


def per_device(
    queries,
    new_keys,
    new_values,
    key_pool,
    value_pool,
    page_table,
    lengths,
    timesteps,
    gate_table,
    out_weight,
    residual,
):
    req_dev = page_table.shape[0]
    group_tok = queries.shape[0]
    new_count = group_tok // req_dev
    share = residual.shape[0]
    groups = residual.shape[1]
    col_count = out_weight.shape[1]
    y_hi, cores = (lax.axis_size(name) for name in ("y_hi", "core"))
    tensor_len = lax.axis_size("x") * lax.axis_size("y_lo")
    own_columns = jnp.broadcast_to(out_weight.T[None], (y_hi * cores, col_count, out_weight.shape[0]))
    weight = lax.all_to_all(own_columns, ("y_hi", "core"), 0, 0, tiled=True)
    weight = weight.reshape(-1, out_weight.shape[0])
    attn = attend(queries, new_keys, new_values, key_pool, value_pool, page_table, lengths)
    attn_all = lax.all_gather(attn, "z", axis=0, tiled=True)
    blocks = project(attn_all, weight, y_hi * cores, tensor_len)
    blocks = blocks.reshape(-1, *blocks.shape[2:])
    arrived = lax.all_to_all(blocks, ("y_hi", "core", "x", "y_lo"), 0, 0, tiled=True)
    request_at = lax.axis_index(("x", "y_lo")) * share // new_count
    step_at = lax.dynamic_index_in_dim(timesteps.reshape(groups, req_dev), request_at, 1, False)
    onehot = (step_at[:, None] == jnp.arange(gate_table.shape[0], dtype=jnp.int32)[None, :]).astype(
        jnp.float32
    )
    gate = jnp.dot(onehot, gate_table, precision=lax.Precision.HIGHEST)
    return finish(arrived.reshape(y_hi, cores, tensor_len, *arrived.shape[1:]), gate, residual)


def solution(mesh):
    dp = ("y_hi", "z", "core")
    tensor = ("x", "y_lo")
    split = Mesh(mesh.devices.reshape(2, -1, 2, 4, 2), dp + tensor)
    placed = (
        P(dp, tensor),
        P(dp, tensor),
        P(dp, tensor),
        P(dp, None, tensor),
        P(dp, None, tensor),
        P(dp, None),
        P(dp),
        P(),
        P(None, dp),
        P(tensor, dp),
        P(tensor, None, dp),
    )
    return jax.shard_map(
        per_device, mesh=split, in_specs=placed, out_specs=P(tensor, None, dp), check_vma=False
    )
```
